128 devices in a mesh: grp: 4 (over x_hi, core), vec: 32 (over z, y, x_lo).
Axes of the slice: x: 4 (x_hi: 2, x_lo: 2; x = x_hi * 2 + x_lo), y: 4, z: 4, core: 2. Of those that a mesh axis runs over, the one named last changes fastest.
Arguments:
- vv_vectors: bfloat16 [1280, 1000, 1000], P(('grp', 'vec')), may hold values from -0.1875 to 0.1875
- oo_vectors: bfloat16 [1280, 100, 100], P(('grp', 'vec')), may hold values from -0.625 to 0.625
- ov_slab: bfloat16 [1280, 1024], P(('grp', 'vec')), may hold values from -0.15625 to 0.15625
- amplitudes: bfloat16 [100, 1000], P('grp'), may hold values from -6 to 6
Outputs:
- sigma_slab: float32 [96000, 1024], P(('grp', 'vec'))
The draws below stay inside these ranges and needn't reach their ends.
All inputs are finite; a program needn't handle non-finite values.
Results may differ from the reference program's by a relative error of at most 0.0029.
Values may be sent and summed in bfloat16 or wider, within the bound.
No kernel may reach another device: no remote copies, remote signals or barrier semaphores. Data moves between devices by JAX's collectives and lax.ppermute only.
A program may use at most 128 MiB of HBM per device.

```python
import math
import jax
import jax.numpy as jnp
from jax import lax

NO = 100
NV = 1000
NP = 1280
I_ROWS = 96
SLAB = 1024


def level_of(key, dims, split, low, largest):
    level = 1.0
    for axis_at, parts in split:
        heights = jax.random.uniform(jax.random.fold_in(jax.random.fold_in(key, 6), axis_at), (parts,), jnp.float32, low / len(split), largest / len(split))
        level = level * jnp.repeat(jnp.exp(heights), dims[axis_at] // parts).reshape((-1,) + (1,) * (len(dims) - 1 - axis_at))
    return level


def gaussian(own_key, extent, scale, reach, shards=(), held_as=jnp.bfloat16):
    entries = jax.random.normal(own_key, extent, jnp.float32) * scale
    if len(shards) > 0:
        entries = level_of(own_key, extent, shards, -0.22, 0.18) * entries
    return jnp.clip(entries, min=-reach, max=reach).astype(held_as)


def setup_inputs(seed: int = 0) -> dict:
    keys = jax.random.split(jax.random.key(seed), 5)
    vv_vectors = gaussian(keys[0], (NP, NV, NV), NV ** -0.5, 0.1875, ((0, 128),))
    oo_vectors = gaussian(keys[1], (NP, NO, NO), NO ** -0.5, 0.625, ((0, 128),))
    ov_slab = gaussian(keys[2], (NP, SLAB), NP ** -0.5, 0.15625, ((0, 128),))
    amplitudes = gaussian(keys[3], (NO, NV), 1.0, 6.0, ((0, 4),))
    return {"vv_vectors": vv_vectors, "oo_vectors": oo_vectors, "ov_slab": ov_slab, "amplitudes": amplitudes}


def reference(vv_vectors, oo_vectors, ov_slab, amplitudes):
    block_size = math.gcd(NP, 64)
    window = amplitudes[:I_ROWS].astype(jnp.float32)
    amps_all = amplitudes.astype(jnp.float32)

    def accumulate(running, counter):
        offset = (counter * block_size).astype(jnp.int32)
        vv_block = lax.dynamic_slice_in_dim(vv_vectors, offset, block_size, 0).astype(jnp.float32)
        oo_block = lax.dynamic_slice_in_dim(oo_vectors, offset, block_size, 0)[:, :, :I_ROWS].astype(jnp.float32)
        ov_part = lax.dynamic_slice_in_dim(ov_slab, offset, block_size, 0)
        direct_term = jnp.einsum('ib,pab->pia', window, vv_block)
        hole_term = jnp.einsum('pji,ja->pia', oo_block, amps_all)
        dressed = (direct_term - hole_term).astype(jnp.bfloat16).reshape(block_size, I_ROWS * NV)
        update = lax.dot_general(dressed, ov_part, (((0,), (0,)), ((), ())), preferred_element_type=jnp.float32)
        return running + update, None

    start_sum = jnp.zeros((I_ROWS * NV, SLAB), jnp.float32)
    running, _ = lax.scan(accumulate, start_sum, jnp.arange(NP // block_size, dtype=jnp.int32))
    return running
```

```python
import jax
import jax.numpy as jnp
from jax import lax
from jax.experimental import pallas as pl
from jax.experimental.pallas import tpu as pltpu
from jax.sharding import Mesh, PartitionSpec as P

NO = 100
NV = 1000
I_ROWS = 96
SLAB = 1024
DEVICES = 128
LOCAL = 10
QUARTER = 250
BLOCK = 32
WIDE = 256
AXES = ("x_hi", "core", "z", "y", "x_lo")
RING = ("z", "y", "x_hi", "x_lo", "core")
F32 = jnp.float32
BF16 = jnp.bfloat16


def offset_of(piece):
    return (QUARTER * piece) % WIDE


def dress_kernel(vv_ref, oo_ref, amps_ref, out_ref, window, wide, blocks):
    p = pl.program_id(0)
    row = lax.broadcasted_iota(jnp.int32, (I_ROWS, NO), 0)
    col = lax.broadcasted_iota(jnp.int32, (I_ROWS, NO), 1)
    pick = jnp.where(col == 3 * (row % 32) + row // 32, 1.0, 0.0).astype(BF16)

    @pl.when(p == 0)
    def _():
        window[...] = jnp.dot(pick, amps_ref[...], preferred_element_type=F32).astype(BF16)
        wide[...] = jnp.zeros_like(wide)
        blocks[...] = jnp.zeros_like(blocks)

    direct = lax.dot_general(
        window[...], vv_ref[0], (((1,), (1,)), ((), ())), preferred_element_type=F32
    )
    holes = lax.dot_general(
        pick, oo_ref[0], (((1,), (1,)), ((), ())), preferred_element_type=F32
    ).astype(BF16)
    hole = jnp.dot(holes, amps_ref[...], preferred_element_type=F32)
    wide[:, :NV] = direct - hole

    lane = lax.broadcasted_iota(jnp.int32, (32, WIDE), 1)
    for t in range(3):
        for q in range(4):
            block, s = divmod(4 * t + q, 3)
            low = min(QUARTER * q // 128 * 128, 512)
            shift = (offset_of(s) - (QUARTER * q - low)) % 512
            part = wide[32 * t : 32 * (t + 1), low : low + 512]
            if shift:
                part = pltpu.roll(part, shift, 1)
            if s:
                part = jnp.where(lane >= offset_of(s), part[:, :WIDE], part[:, WIDE:])
            else:
                part = part[:, :WIDE]
            start = BLOCK * block + jnp.where(p < 8, 8 * s + p, 16 + 2 * s + p)
            for half in range(2):
                blocks[half, pl.ds(start, 32, stride=128), :] = part[:, 128 * half : 128 * (half + 1)]

    @pl.when(p == LOCAL - 1)
    def _():
        @pl.loop(0, DEVICES)
        def _(d):
            x_hi, core, z, y, x_lo = d // 64, (d // 32) % 2, (d // 8) % 4, (d // 2) % 4, d % 2
            to = z * 32 + y * 8 + x_hi * 4 + x_lo * 2 + core
            rows = pl.ds(pl.multiple_of(d * BLOCK, BLOCK), BLOCK)
            for half in range(2):
                out_ref[to, :, 128 * half : 128 * (half + 1)] = blocks[half, rows, :].astype(BF16)


def dress(vv_vectors, oo_vectors, amps_all):
    return pl.pallas_call(
        dress_kernel,
        grid=(LOCAL,),
        out_shape=jax.ShapeDtypeStruct((DEVICES, BLOCK, WIDE), BF16),
        in_specs=[
            pl.BlockSpec((1, NV, NV), lambda p: (p, 0, 0)),
            pl.BlockSpec((1, NO, NO), lambda p: (p, 0, 0)),
            pl.BlockSpec((NO, NV), lambda p: (0, 0)),
        ],
        out_specs=pl.BlockSpec((DEVICES, BLOCK, WIDE), lambda p: (0, 0, 0)),
        scratch_shapes=[
            pltpu.VMEM((I_ROWS, NV), BF16),
            pltpu.VMEM((I_ROWS, 1024), F32),
            pltpu.VMEM((2, DEVICES * BLOCK, 128), F32),
        ],
        compiler_params=pltpu.CompilerParams(dimension_semantics=("arbitrary",)),
        cost_estimate=pl.CostEstimate(
            flops=2 * LOCAL * I_ROWS * NV * NV, bytes_accessed=2 * LOCAL * NV * NV, transcendentals=0
        ),
        name="dress",
    )(vv_vectors, oo_vectors, amps_all)


def contract_kernel(blocks_ref, slab_ref, out_ref, dressed, slab, tail, slab_tail):
    GROUP = 16
    m = pl.program_id(0)

    @pl.when(m == 0)
    def _():
        lane = lax.broadcasted_iota(jnp.int32, (GROUP * 8, WIDE), 1)

        @pl.loop(0, DEVICES // GROUP)
        def _(g):
            group = pl.ds(g * GROUP, GROUP)
            rows = pl.ds(pl.multiple_of(g * GROUP * 8, GROUP * 8), GROUP * 8)
            parts = [
                blocks_ref[group, 8 * s : 8 * s + 8, :].astype(F32).reshape(GROUP * 8, WIDE)
                for s in range(4)
            ]
            dressed[rows, 0:256] = jnp.where(lane < 250, parts[0], parts[1]).astype(BF16)
            dressed[rows, 256:512] = jnp.where(lane < 244, parts[1], parts[2]).astype(BF16)
            dressed[rows, 512:768] = parts[2].astype(BF16)
            for half in range(2):
                tail[half, rows, :] = parts[3][:, 128 * half : 128 * (half + 1)]
            for c in range(8):
                cols = slice(128 * c, 128 * (c + 1))
                slab[rows, cols] = (
                    slab_ref[group, 8 * c : 8 * c + 8, :].astype(F32).reshape(GROUP * 8, 128).astype(BF16)
                )
            tails = pl.ds(pl.multiple_of(g * GROUP * 16, GROUP * 16), GROUP * 16)
            slab_tail[tails, :] = slab_ref[group, 64:80, :].astype(F32).reshape(GROUP * 16, 128)

        lanes = lax.broadcasted_iota(jnp.int32, (DEVICES, 128), 1) + 128
        for e in range(2):
            rows = slice(1024 + 128 * e, 1152 + 128 * e)
            for half in range(2):
                parts = [tail[half, pl.ds(2 * s + e, DEVICES, stride=8), :] for s in range(3)]
                if half:
                    first = jnp.where(lanes < 250, parts[0], parts[1])
                    second = jnp.where(lanes < 244, parts[1], parts[2])
                else:
                    first, second = parts[0], parts[1]
                for k, part in enumerate((first, second, parts[2])):
                    at = 256 * k + 128 * half
                    dressed[rows, at : at + 128] = part.astype(BF16)
            for c in range(8):
                slab[rows, 128 * c : 128 * (c + 1)] = slab_tail[
                    pl.ds(8 * e + c, DEVICES, stride=16), :
                ].astype(BF16)

    mine = dressed[:, pl.ds(pl.multiple_of(m * WIDE, WIDE), WIDE)]
    out_ref[...] = lax.dot_general(
        mine, slab[...], (((0,), (0,)), ((), ())), preferred_element_type=F32
    )


def contract(blocks, slabs):
    return pl.pallas_call(
        contract_kernel,
        grid=(3,),
        out_shape=jax.ShapeDtypeStruct((750, SLAB), F32),
        in_specs=[
            pl.BlockSpec((DEVICES, BLOCK, WIDE), lambda m: (0, 0, 0)),
            pl.BlockSpec((DEVICES, 80, 128), lambda m: (0, 0, 0)),
        ],
        out_specs=pl.BlockSpec((WIDE, SLAB), lambda m: (m, 0)),
        scratch_shapes=[
            pltpu.VMEM((1280, 768), BF16),
            pltpu.VMEM((1280, SLAB), BF16),
            pltpu.VMEM((2, 1024, 128), F32),
            pltpu.VMEM((2048, 128), F32),
        ],
        compiler_params=pltpu.CompilerParams(dimension_semantics=("arbitrary",)),
        cost_estimate=pl.CostEstimate(
            flops=2 * 768 * 1280 * SLAB, bytes_accessed=8 * 1024 * 1024, transcendentals=0
        ),
        name="contract",
    )(blocks, slabs)


def slab_rows(ov_slab):
    head = ov_slab[:8].reshape(8, 8, 128).transpose(1, 0, 2).reshape(64, 128)
    return jnp.concatenate([head, ov_slab[8:].reshape(16, 128)], axis=0)


def shards(vv_vectors, oo_vectors, ov_slab, amplitudes):
    slabs = lax.all_gather(slab_rows(ov_slab), RING, axis=0, tiled=False)
    amps_all = lax.all_gather(amplitudes, ("x_hi", "core"), axis=0, tiled=True)
    blocks = dress(vv_vectors, oo_vectors, amps_all)
    blocks = lax.all_to_all(blocks, RING, split_axis=0, concat_axis=0, tiled=True)
    return contract(blocks, slabs)


def solution(mesh):
    split = Mesh(mesh.devices.reshape(2, 2, 4, 4, 2), AXES)
    return jax.shard_map(
        shards,
        mesh=split,
        in_specs=(P(AXES, None, None), P(AXES, None, None), P(AXES, None), P(("x_hi", "core"), None)),
        out_specs=P(AXES, None),
        check_vma=False,
    )
```

```python
import jax
import jax.numpy as jnp
from jax import lax
from jax.experimental import pallas as pl
from jax.experimental.pallas import tpu as pltpu
from jax.sharding import Mesh, PartitionSpec as P

NO = 100
NV = 1000
I_ROWS = 96
SLAB = 1024
DEVICES = 128
LOCAL = 10
QUARTER = 250
BLOCK = 32
WIDE = 256
AXES = ("x_hi", "core", "z", "y", "x_lo")
RING = ("z", "y", "x_hi", "x_lo", "core")
F32 = jnp.float32
BF16 = jnp.bfloat16


def offset_of(piece):
    return (QUARTER * piece) % WIDE


def dress_kernel(vv_hbm, oo_hbm, amps_0, amps_1, amps_2, amps_3, out_hbm, vv, oo, quarters, spread, amps, window, holes, wide, blocks, out, vv_sem, in_sem, out_sem):
    small = [
        pltpu.make_async_copy(piece, quarters.at[d], in_sem.at[d])
        for d, piece in enumerate((amps_0, amps_1, amps_2, amps_3))
    ]
    small.append(pltpu.make_async_copy(oo_hbm, oo, in_sem.at[4]))
    large = [pltpu.make_async_copy(vv_hbm.at[p], vv.at[p], vv_sem.at[p]) for p in range(LOCAL)]
    for copy in small + large:
        copy.start()

    row = lax.broadcasted_iota(jnp.int32, (I_ROWS, NO), 0)
    col = lax.broadcasted_iota(jnp.int32, (I_ROWS, NO), 1)
    pick = jnp.where(col == 3 * (row % 32) + row // 32, 1.0, 0.0).astype(BF16)
    wide[:, :, 896:1024] = jnp.zeros((2, I_ROWS, 128), F32)
    for half in range(2):
        for spare in range(2):
            blocks[half, pl.ds(30 + spare, DEVICES, stride=BLOCK), :] = jnp.zeros((DEVICES, 128), F32)
    spread[...] = jnp.zeros_like(spread)
    for copy in small:
        copy.wait()
    for d in range(4):
        spread[32 * d : 32 * d + 25, :] = quarters[d]
    me = lax.axis_index(("x_hi", "core"))
    into, at = (lax.broadcasted_iota(jnp.int32, (NO, 128), axis) for axis in (0, 1))
    place = jnp.where((into == 25 * (me ^ (at // 32)) + at % 32) & (at % 32 < 25), 1.0, 0.0).astype(BF16)
    amps[...] = jnp.dot(place, spread[...], preferred_element_type=F32).astype(BF16)
    window[...] = jnp.dot(pick, amps[...], preferred_element_type=F32).astype(BF16)
    for p in range(LOCAL):
        holes[p] = lax.dot_general(
            pick, oo[p], (((1,), (1,)), ((), ())), preferred_element_type=F32
        ).astype(BF16)

    lane = lax.broadcasted_iota(jnp.int32, (32, WIDE), 1)

    def scatter(p):
        for t in range(3):
            for q in range(4):
                block, s = divmod(4 * t + q, 3)
                low = min(QUARTER * q // 128 * 128, 512)
                shift = (offset_of(s) - (QUARTER * q - low)) % 512
                part = wide[p % 2, 32 * t : 32 * (t + 1), low : low + 512]
                if shift:
                    part = pltpu.roll(part, shift, 1)
                if s:
                    part = jnp.where(lane >= offset_of(s), part[:, :WIDE], part[:, WIDE:])
                else:
                    part = part[:, :WIDE]
                start = BLOCK * block + (8 * s + p if p < 8 else 16 + 2 * s + p)
                for half in range(2):
                    blocks[half, pl.ds(start, 32, stride=128), :] = part[:, 128 * half : 128 * (half + 1)]

    for p in range(LOCAL):
        large[p].wait()
        direct = lax.dot_general(
            window[...], vv[p], (((1,), (1,)), ((), ())), preferred_element_type=F32
        )
        hole = jnp.dot(holes[p], amps[...], preferred_element_type=F32)
        wide[p % 2, :, :NV] = direct - hole
        if p:
            scatter(p - 1)
    scatter(LOCAL - 1)

    sends = []
    for chunk in range(8):
        for to in range(16 * chunk, 16 * (chunk + 1)):
            z, y, x_hi, x_lo, core = to // 32, to // 8 % 4, to // 4 % 2, to // 2 % 2, to % 2
            at = BLOCK * (x_hi * 64 + core * 32 + z * 8 + y * 2 + x_lo)
            for half in range(2):
                out[to, :, 128 * half : 128 * (half + 1)] = blocks[half, at : at + BLOCK, :].astype(BF16)
        piece = pl.ds(16 * chunk, 16)
        sends.append(pltpu.make_async_copy(out.at[piece], out_hbm.at[piece], out_sem.at[chunk]))
        sends[-1].start()
    for copy in sends:
        copy.wait()


def dress(vv_vectors, oo_vectors, quarters):
    anywhere = pl.BlockSpec(memory_space=pl.ANY)
    held = pl.BlockSpec(memory_space=pltpu.HBM)
    return pl.pallas_call(
        dress_kernel,
        out_shape=jax.ShapeDtypeStruct((DEVICES, BLOCK, WIDE), BF16),
        in_specs=[held, held] + [anywhere] * 4,
        out_specs=held,
        scratch_shapes=[
            pltpu.VMEM((LOCAL, NV, NV), BF16),
            pltpu.VMEM((LOCAL, NO, NO), BF16),
            pltpu.VMEM((4, 25, NV), BF16),
            pltpu.VMEM((128, NV), BF16),
            pltpu.VMEM((NO, NV), BF16),
            pltpu.VMEM((I_ROWS, NV), BF16),
            pltpu.VMEM((LOCAL, I_ROWS, NO), BF16),
            pltpu.VMEM((2, I_ROWS, 1024), F32),
            pltpu.VMEM((2, DEVICES * BLOCK, 128), F32),
            pltpu.VMEM((DEVICES, BLOCK, WIDE), BF16),
            pltpu.SemaphoreType.DMA((LOCAL,)),
            pltpu.SemaphoreType.DMA((5,)),
            pltpu.SemaphoreType.DMA((8,)),
        ],
        compiler_params=pltpu.CompilerParams(vmem_limit_bytes=48 * 1024 * 1024),
        cost_estimate=pl.CostEstimate(
            flops=2 * LOCAL * I_ROWS * NV * NV, bytes_accessed=2 * LOCAL * NV * NV, transcendentals=0
        ),
        name="dress",
    )(vv_vectors, oo_vectors, *quarters)


def source(n):
    z, y, x, core = (lax.axis_index(a) for a in ("z", "y", ("x_hi", "x_lo"), "core"))
    to_z, to_y, to_x = n % 4, n // 4 % 4, n // 16 % 4
    from_z, from_y, from_x = (z + 4 - to_z) % 4, (y + 4 - to_y) % 4, (x + 4 - to_x) % 4
    return from_z * 32 + from_y * 8 + from_x * 2 + (core + n // 64) % 2


def assemble_kernel(blocks_ref, out_ref, tail):
    lane = lax.broadcasted_iota(jnp.int32, (16, WIDE), 1)

    @pl.loop(0, DEVICES // 16)
    def _(g):
        for pair in range(8):
            n = g * 16 + 2 * pair
            one, two = source(n), source(n + 1)
            parts = [
                jnp.concatenate(
                    [
                        blocks_ref[one, 8 * s : 8 * s + 8, :].astype(F32),
                        blocks_ref[two, 8 * s : 8 * s + 8, :].astype(F32),
                    ],
                    axis=0,
                )
                for s in range(4)
            ]
            rows = pl.ds(pl.multiple_of(n * 8, 16), 16)
            out_ref[rows, 0:256] = jnp.where(lane < 250, parts[0], parts[1]).astype(BF16)
            out_ref[rows, 256:512] = jnp.where(lane < 244, parts[1], parts[2]).astype(BF16)
            out_ref[rows, 512:768] = parts[2].astype(BF16)
            for half in range(2):
                tail[half, rows, :] = parts[3][:, 128 * half : 128 * (half + 1)]

    lanes = lax.broadcasted_iota(jnp.int32, (DEVICES, 128), 1) + 128
    for e in range(2):
        rows = slice(1024 + 128 * e, 1152 + 128 * e)
        for half in range(2):
            parts = [tail[half, pl.ds(2 * s + e, DEVICES, stride=8), :] for s in range(3)]
            if half:
                first = jnp.where(lanes < 250, parts[0], parts[1])
                second = jnp.where(lanes < 244, parts[1], parts[2])
            else:
                first, second = parts[0], parts[1]
            for k, part in enumerate((first, second, parts[2])):
                at = 256 * k + 128 * half
                out_ref[rows, at : at + 128] = part.astype(BF16)


def assemble(blocks):
    return pl.pallas_call(
        assemble_kernel,
        out_shape=jax.ShapeDtypeStruct((1280, 768), BF16),
        scratch_shapes=[pltpu.VMEM((2, 1024, 128), F32)],
        compiler_params=pltpu.CompilerParams(vmem_limit_bytes=24 * 1024 * 1024),
        cost_estimate=pl.CostEstimate(flops=0, bytes_accessed=4 * 1024 * 1024, transcendentals=0),
        name="assemble",
    )(blocks)


def contract_kernel(dressed_ref, mine_ref, other_ref, out_ref, slab, slab_tail):
    GROUP = 16
    m = pl.program_id(0)

    @pl.when(m == 0)
    def _():
        for which, slab_ref in enumerate((mine_ref, other_ref)):

            @pl.loop(0, 64 // GROUP)
            def _(g):
                group = pl.ds(g * GROUP, GROUP)
                at = (64 * which + g * GROUP) * 8
                rows = pl.ds(pl.multiple_of(at, GROUP * 8), GROUP * 8)
                for c in range(8):
                    cols = slice(128 * c, 128 * (c + 1))
                    slab[rows, cols] = (
                        slab_ref[group, 8 * c : 8 * c + 8, :].astype(F32).reshape(GROUP * 8, 128).astype(BF16)
                    )
                tails = pl.ds(pl.multiple_of(2 * at, GROUP * 16), GROUP * 16)
                slab_tail[tails, :] = slab_ref[group, 64:80, :].astype(F32).reshape(GROUP * 16, 128)

        for e in range(2):
            rows = slice(1024 + 128 * e, 1152 + 128 * e)
            for c in range(8):
                slab[rows, 128 * c : 128 * (c + 1)] = slab_tail[
                    pl.ds(8 * e + c, DEVICES, stride=16), :
                ].astype(BF16)

    out_ref[...] = lax.dot_general(
        dressed_ref[...], slab[...], (((0,), (0,)), ((), ())), preferred_element_type=F32
    )


def contract(dressed, mine, other):
    return pl.pallas_call(
        contract_kernel,
        grid=(3,),
        out_shape=jax.ShapeDtypeStruct((750, SLAB), F32),
        in_specs=[
            pl.BlockSpec((1280, WIDE), lambda m: (0, m)),
            pl.BlockSpec((64, 80, 128), lambda m: (0, 0, 0)),
            pl.BlockSpec((64, 80, 128), lambda m: (0, 0, 0)),
        ],
        out_specs=pl.BlockSpec((WIDE, SLAB), lambda m: (m, 0)),
        scratch_shapes=[pltpu.VMEM((1280, SLAB), BF16), pltpu.VMEM((2048, 128), F32)],
        compiler_params=pltpu.CompilerParams(
            dimension_semantics=("arbitrary",), vmem_limit_bytes=32 * 1024 * 1024
        ),
        cost_estimate=pl.CostEstimate(
            flops=2 * 768 * 1280 * SLAB, bytes_accessed=8 * 1024 * 1024, transcendentals=0
        ),
        name="contract",
    )(dressed, mine, other)


def slab_kernel(slab_ref, out_ref, rows):
    for c in range(8):
        part = slab_ref[:, 128 * c : 128 * (c + 1)].astype(F32)
        rows[8 * c : 8 * c + 8, :] = part[0:8]
        for e in range(2):
            rows[64 + 8 * e + c : 65 + 8 * e + c, :] = part[8 + e : 9 + e]
    out_ref[...] = rows[...].astype(BF16)


def slab_rows(ov_slab):
    return pl.pallas_call(
        slab_kernel,
        out_shape=jax.ShapeDtypeStruct((80, 128), BF16),
        scratch_shapes=[pltpu.VMEM((80, 128), F32)],
        compiler_params=pltpu.CompilerParams(vmem_limit_bytes=4 * 1024 * 1024),
        cost_estimate=pl.CostEstimate(flops=0, bytes_accessed=64 * 1024, transcendentals=0),
        name="slab_rows",
    )(ov_slab)


def round_axis(rows, axis):
    others = [lax.ppermute(rows, axis, [(i, (i + d) % 4) for i in range(4)]) for d in (1, 2, 3)]
    return jnp.concatenate([rows, *others], axis=0)


def shards(vv_vectors, oo_vectors, ov_slab, amplitudes):
    group = ("x_hi", "core")
    quarters = [amplitudes] + [lax.ppermute(amplitudes, group, [(i, i ^ d) for i in range(4)]) for d in (1, 2, 3)]
    rows = round_axis(slab_rows(ov_slab), "z")
    rows, quarters = lax.optimization_barrier((rows, quarters))
    rows = round_axis(rows, "y")
    blocks = dress(vv_vectors, oo_vectors, quarters)
    rows, blocks = lax.optimization_barrier((rows, blocks))
    blocks = lax.all_to_all(blocks, RING, split_axis=0, concat_axis=0, tiled=True)
    rows = round_axis(rows, ("x_hi", "x_lo"))
    other = lax.ppermute(rows, "core", [(0, 1), (1, 0)])
    return contract(assemble(blocks), rows.reshape(64, 80, 128), other.reshape(64, 80, 128))


def solution(mesh):
    split = Mesh(mesh.devices.reshape(2, 2, 4, 4, 2), AXES)
    return jax.shard_map(
        shards,
        mesh=split,
        in_specs=(P(AXES, None, None), P(AXES, None, None), P(AXES, None), P(("x_hi", "core"), None)),
        out_specs=P(AXES, None),
        check_vma=False,
    )
```

```python
import jax
import jax.numpy as jnp
from jax import lax
from jax.experimental import pallas as pl
from jax.experimental.pallas import tpu as pltpu
from jax.sharding import Mesh, PartitionSpec as P

NO = 100
NV = 1000
I_ROWS = 96
SLAB = 1024
DEVICES = 128
LOCAL = 10
QUARTER = 250
DRESS_VMEM = 48 * 1024 * 1024
BLOCK = 32
WIDE = 256
AXES = ("x_hi", "core", "z", "y", "x_lo")
RING = ("z", "y", "x_hi", "x_lo", "core")
F32 = jnp.float32
BF16 = jnp.bfloat16


def offset_of(piece):
    return (QUARTER * piece) % WIDE


def picked_rows():
    row = lax.broadcasted_iota(jnp.int32, (I_ROWS, NO), 0)
    col = lax.broadcasted_iota(jnp.int32, (I_ROWS, NO), 1)
    return jnp.where(col == 3 * (row % 32) + row // 32, 1.0, 0.0).astype(BF16)


def holes_kernel(oo_ref, out_ref):
    pick = picked_rows()
    for p in range(LOCAL):
        out_ref[p] = lax.dot_general(
            pick, oo_ref[p], (((1,), (1,)), ((), ())), preferred_element_type=F32
        ).astype(BF16)


def hole_factors(oo_vectors):
    return pl.pallas_call(
        holes_kernel,
        out_shape=jax.ShapeDtypeStruct((LOCAL, I_ROWS, NO), BF16),
        compiler_params=pltpu.CompilerParams(vmem_limit_bytes=4 * 1024 * 1024),
        cost_estimate=pl.CostEstimate(flops=2 * LOCAL * NO**3, bytes_accessed=512 * 1024, transcendentals=0),
        name="hole_factors",
    )(oo_vectors)


def dress_kernel(vv_hbm, holes_hbm, amps_0, amps_1, amps_2, amps_3, out_hbm, vv, holes, quarters, spread, amps, window, wide, blocks, out, vv_sem, in_sem, out_sem):
    small = [
        pltpu.make_async_copy(piece, quarters.at[d], in_sem.at[d])
        for d, piece in enumerate((amps_0, amps_1, amps_2, amps_3))
    ]
    small.append(pltpu.make_async_copy(holes_hbm, holes, in_sem.at[4]))
    large = [pltpu.make_async_copy(vv_hbm.at[p], vv.at[p], vv_sem.at[p]) for p in range(LOCAL)]
    for copy in small + large:
        copy.start()

    pick = picked_rows()
    wide[:, :, 896:1024] = jnp.zeros((2, I_ROWS, 128), F32)
    for half in range(2):
        for spare in range(2):
            blocks[half, pl.ds(30 + spare, DEVICES, stride=BLOCK), :] = jnp.zeros((DEVICES, 128), F32)
    spread[...] = jnp.zeros_like(spread)
    for copy in small:
        copy.wait()
    for d in range(4):
        spread[32 * d : 32 * d + 25, :] = quarters[d]
    me = lax.axis_index(("x_hi", "core"))
    into, at = (lax.broadcasted_iota(jnp.int32, (NO, 128), axis) for axis in (0, 1))
    place = jnp.where((into == 25 * (me ^ (at // 32)) + at % 32) & (at % 32 < 25), 1.0, 0.0).astype(BF16)
    amps[...] = jnp.dot(place, spread[...], preferred_element_type=F32).astype(BF16)
    window[...] = jnp.dot(pick, amps[...], preferred_element_type=F32).astype(BF16)

    lane = lax.broadcasted_iota(jnp.int32, (32, WIDE), 1)

    def scatter(p):
        for t in range(3):
            for q in range(4):
                block, s = divmod(4 * t + q, 3)
                low = min(QUARTER * q // 128 * 128, 512)
                shift = (offset_of(s) - (QUARTER * q - low)) % 512
                part = wide[p % 2, 32 * t : 32 * (t + 1), low : low + 512]
                if shift:
                    part = pltpu.roll(part, shift, 1)
                if s:
                    part = jnp.where(lane >= offset_of(s), part[:, :WIDE], part[:, WIDE:])
                else:
                    part = part[:, :WIDE]
                start = BLOCK * block + (8 * s + p if p < 8 else 16 + 2 * s + p)
                for half in range(2):
                    blocks[half, pl.ds(start, 32, stride=128), :] = part[:, 128 * half : 128 * (half + 1)]

    for p in range(LOCAL):
        large[p].wait()
        direct = lax.dot_general(
            window[...], vv[p], (((1,), (1,)), ((), ())), preferred_element_type=F32
        )
        hole = jnp.dot(holes[p], amps[...], preferred_element_type=F32)
        wide[p % 2, :, :NV] = direct - hole
        if p:
            scatter(p - 1)
    scatter(LOCAL - 1)

    sends = []
    for chunk in range(8):
        for to in range(16 * chunk, 16 * (chunk + 1)):
            z, y, x_hi, x_lo, core = to // 32, to // 8 % 4, to // 4 % 2, to // 2 % 2, to % 2
            at = BLOCK * (x_hi * 64 + core * 32 + z * 8 + y * 2 + x_lo)
            for half in range(2):
                out[to, :, 128 * half : 128 * (half + 1)] = blocks[half, at : at + BLOCK, :].astype(BF16)
        piece = pl.ds(16 * chunk, 16)
        sends.append(pltpu.make_async_copy(out.at[piece], out_hbm.at[piece], out_sem.at[chunk]))
        sends[-1].start()
    for copy in sends:
        copy.wait()


def dress(vv_vectors, holes, quarters):
    anywhere = pl.BlockSpec(memory_space=pl.ANY)
    held = pl.BlockSpec(memory_space=pltpu.HBM)
    return pl.pallas_call(
        dress_kernel,
        out_shape=jax.ShapeDtypeStruct((DEVICES, BLOCK, WIDE), BF16),
        in_specs=[held, held] + [anywhere] * 4,
        out_specs=held,
        scratch_shapes=[
            pltpu.VMEM((LOCAL, NV, NV), BF16),
            pltpu.VMEM((LOCAL, I_ROWS, NO), BF16),
            pltpu.VMEM((4, 25, NV), BF16),
            pltpu.VMEM((128, NV), BF16),
            pltpu.VMEM((NO, NV), BF16),
            pltpu.VMEM((I_ROWS, NV), BF16),
            pltpu.VMEM((2, I_ROWS, 1024), F32),
            pltpu.VMEM((2, DEVICES * BLOCK, 128), F32),
            pltpu.VMEM((DEVICES, BLOCK, WIDE), BF16),
            pltpu.SemaphoreType.DMA((LOCAL,)),
            pltpu.SemaphoreType.DMA((5,)),
            pltpu.SemaphoreType.DMA((8,)),
        ],
        compiler_params=pltpu.CompilerParams(vmem_limit_bytes=DRESS_VMEM),
        cost_estimate=pl.CostEstimate(
            flops=2 * LOCAL * I_ROWS * NV * NV, bytes_accessed=2 * LOCAL * NV * NV, transcendentals=0
        ),
        name="dress",
    )(vv_vectors, holes, *quarters)


def order_kernel(mine_ref, other_ref, out_ref, tail):
    me_z, me_y, me_x, me_core = (lax.axis_index(a) for a in ("z", "y", ("x_hi", "x_lo"), "core"))

    @pl.loop(0, DEVICES // 2)
    def _(chip):
        z, y, x = chip // 16, chip // 4 % 4, chip % 4
        at = (me_x + 4 - x) % 4 * 16 + (me_y + 4 - y) % 4 * 4 + (me_z + 4 - z) % 4
        mine, other = mine_ref[at].astype(F32), other_ref[at].astype(F32)
        one, two = jnp.where(me_core == 0, mine, other), jnp.where(me_core == 0, other, mine)
        rows = pl.ds(pl.multiple_of(chip * 16, 16), 16)
        for c in range(8):
            both = jnp.concatenate([one[8 * c : 8 * c + 8], two[8 * c : 8 * c + 8]], axis=0)
            out_ref[rows, 128 * c : 128 * (c + 1)] = both.astype(BF16)
        start = pl.multiple_of(chip * 32, 32)
        tail[pl.ds(start, 16), :] = one[64:80]
        tail[pl.ds(start + 16, 16), :] = two[64:80]

    for e in range(2):
        for c in range(8):
            out_ref[1024 + 128 * e : 1152 + 128 * e, 128 * c : 128 * (c + 1)] = tail[
                pl.ds(8 * e + c, DEVICES, stride=16), :
            ].astype(BF16)


def ordered(mine, other):
    return pl.pallas_call(
        order_kernel,
        out_shape=jax.ShapeDtypeStruct((1280, SLAB), BF16),
        scratch_shapes=[pltpu.VMEM((2048, 128), F32)],
        compiler_params=pltpu.CompilerParams(vmem_limit_bytes=16 * 1024 * 1024),
        cost_estimate=pl.CostEstimate(flops=0, bytes_accessed=6 * 1024 * 1024, transcendentals=0),
        name="ordered",
    )(mine, other)


def contract_kernel(blocks_ref, slab_ref, out_ref, dressed, tail):
    GROUP = 16
    m = pl.program_id(0)
    after = jnp.minimum(m + 1, 2)
    limit = jnp.where(m < 2, 250 - 6 * m, WIDE)

    @pl.when(m == 0)
    def _():
        @pl.loop(0, DEVICES // GROUP, unroll=2)
        def _(g):
            group = pl.ds(g * GROUP, GROUP)
            rows = pl.ds(pl.multiple_of(g * GROUP * 8, GROUP * 8), GROUP * 8)
            for half in range(2):
                part = blocks_ref[group, 24:32, 128 * half : 128 * (half + 1)]
                tail[half, rows, :] = part.astype(F32).reshape(GROUP * 8, 128)

    lane = lax.broadcasted_iota(jnp.int32, (GROUP * 8, WIDE), 1)

    @pl.loop(0, DEVICES // GROUP, unroll=2)
    def _(g):
        group = pl.ds(g * GROUP, GROUP)
        rows = pl.ds(pl.multiple_of(g * GROUP * 8, GROUP * 8), GROUP * 8)
        one, two = (
            blocks_ref[group, pl.ds(pl.multiple_of(8 * s, 8), 8), :].astype(F32).reshape(GROUP * 8, WIDE)
            for s in (m, after)
        )
        dressed[rows, :] = jnp.where(lane < limit, one, two).astype(BF16)

    lanes = lax.broadcasted_iota(jnp.int32, (DEVICES, 128), 1)
    for e in range(2):
        rows = slice(1024 + 128 * e, 1152 + 128 * e)
        for half in range(2):
            one, two = (tail[half, pl.ds(2 * s + e, DEVICES, stride=8), :] for s in (m, after))
            dressed[rows, 128 * half : 128 * (half + 1)] = jnp.where(
                lanes + 128 * half < limit, one, two
            ).astype(BF16)

    out_ref[...] = lax.dot_general(
        dressed[...], slab_ref[...], (((0,), (0,)), ((), ())), preferred_element_type=F32
    )


def contract(blocks, slab):
    return pl.pallas_call(
        contract_kernel,
        grid=(3,),
        out_shape=jax.ShapeDtypeStruct((750, SLAB), F32),
        in_specs=[
            pl.BlockSpec(memory_space=pltpu.VMEM),
            pl.BlockSpec(memory_space=pltpu.VMEM),
        ],
        out_specs=pl.BlockSpec((WIDE, SLAB), lambda m: (m, 0)),
        scratch_shapes=[pltpu.VMEM((1280, WIDE), BF16), pltpu.VMEM((2, 1024, 128), F32)],
        compiler_params=pltpu.CompilerParams(
            dimension_semantics=("arbitrary",), vmem_limit_bytes=32 * 1024 * 1024
        ),
        cost_estimate=pl.CostEstimate(
            flops=2 * 768 * 1280 * SLAB, bytes_accessed=8 * 1024 * 1024, transcendentals=0
        ),
        name="contract",
    )(blocks, slab)


def slab_kernel(slab_ref, out_ref, rows):
    for c in range(8):
        part = slab_ref[:, 128 * c : 128 * (c + 1)].astype(F32)
        rows[8 * c : 8 * c + 8, :] = part[0:8]
        for e in range(2):
            rows[64 + 8 * e + c : 65 + 8 * e + c, :] = part[8 + e : 9 + e]
    out_ref[...] = rows[...].astype(BF16)


def slab_rows(ov_slab):
    return pl.pallas_call(
        slab_kernel,
        out_shape=jax.ShapeDtypeStruct((80, 128), BF16),
        scratch_shapes=[pltpu.VMEM((80, 128), F32)],
        compiler_params=pltpu.CompilerParams(vmem_limit_bytes=4 * 1024 * 1024),
        cost_estimate=pl.CostEstimate(flops=0, bytes_accessed=64 * 1024, transcendentals=0),
        name="slab_rows",
    )(ov_slab)


def round_axis(rows, axis):
    others = [lax.ppermute(rows, axis, [(i, (i + d) % 4) for i in range(4)]) for d in (1, 2, 3)]
    return jnp.concatenate([rows, *others], axis=0)


def shards(vv_vectors, oo_vectors, ov_slab, amplitudes):
    group = ("x_hi", "core")
    quarters = [amplitudes] + [lax.ppermute(amplitudes, group, [(i, i ^ d) for i in range(4)]) for d in (1, 2, 3)]
    rows = round_axis(slab_rows(ov_slab), "z")
    holes = hole_factors(oo_vectors)
    rows, holes, quarters = lax.optimization_barrier((rows, holes, quarters))
    rows = round_axis(rows, "y")
    blocks = dress(vv_vectors, holes, quarters)
    rows, blocks = lax.optimization_barrier((rows, blocks))
    blocks = lax.all_to_all(blocks, RING, split_axis=0, concat_axis=0, tiled=True)
    rows = round_axis(rows, ("x_hi", "x_lo"))
    other = lax.ppermute(rows, "core", [(0, 1), (1, 0)])
    return contract(blocks, ordered(rows.reshape(64, 80, 128), other.reshape(64, 80, 128)))


def solution(mesh):
    split = Mesh(mesh.devices.reshape(2, 2, 4, 4, 2), AXES)
    return jax.shard_map(
        shards,
        mesh=split,
        in_specs=(P(AXES, None, None), P(AXES, None, None), P(AXES, None), P(("x_hi", "core"), None)),
        out_specs=P(AXES, None),
        check_vma=False,
    )
```

```python
import jax
import jax.numpy as jnp
from jax import lax
from jax.experimental import pallas as pl
from jax.experimental.pallas import tpu as pltpu
from jax.sharding import Mesh, PartitionSpec as P

NO = 100
NV = 1000
I_ROWS = 96
SLAB = 1024
DEVICES = 128
LOCAL = 10
QUARTER = 250
DRESS_VMEM = 60 * 1024 * 1024
BLOCK = 32
WIDE = 256
AXES = ("x_hi", "core", "z", "y", "x_lo")
RING = ("core", "z", "y", "x_hi", "x_lo")
F32 = jnp.float32
BF16 = jnp.bfloat16


def offset_of(piece):
    return (QUARTER * piece) % WIDE


def picked_rows():
    row = lax.broadcasted_iota(jnp.int32, (I_ROWS, NO), 0)
    col = lax.broadcasted_iota(jnp.int32, (I_ROWS, NO), 1)
    return jnp.where(col == 3 * (row % 32) + row // 32, 1.0, 0.0).astype(BF16)


def holes_kernel(oo_ref, out_ref):
    pick = picked_rows()
    for p in range(LOCAL):
        out_ref[p] = lax.dot_general(
            pick, oo_ref[p], (((1,), (1,)), ((), ())), preferred_element_type=F32
        ).astype(BF16)


def hole_factors(oo_vectors):
    return pl.pallas_call(
        holes_kernel,
        out_shape=jax.ShapeDtypeStruct((LOCAL, I_ROWS, NO), BF16),
        compiler_params=pltpu.CompilerParams(vmem_limit_bytes=4 * 1024 * 1024),
        cost_estimate=pl.CostEstimate(flops=2 * LOCAL * NO**3, bytes_accessed=512 * 1024, transcendentals=0),
        name="hole_factors",
    )(oo_vectors)


def dress_kernel(vv_hbm, holes_hbm, amps_0, amps_1, amps_2, amps_3, out_hbm, vv, holes, quarters, spread, amps, window, wide, blocks, out, vv_sem, in_sem, out_sem):
    small = [
        pltpu.make_async_copy(piece, quarters.at[d], in_sem.at[d])
        for d, piece in enumerate((amps_0, amps_1, amps_2, amps_3))
    ]
    small.append(pltpu.make_async_copy(holes_hbm, holes, in_sem.at[4]))
    large = [pltpu.make_async_copy(vv_hbm.at[p], vv.at[p], vv_sem.at[p]) for p in range(LOCAL)]
    for copy in small + large[:2]:
        copy.start()

    pick = picked_rows()
    wide[:, :, 896:1024] = jnp.zeros((2, I_ROWS, 128), F32)
    for half in range(2):
        for spare in range(2):
            blocks[half, pl.ds(30 + spare, DEVICES, stride=BLOCK), :] = jnp.zeros((DEVICES, 128), F32)
    spread[...] = jnp.zeros_like(spread)
    for copy in small:
        copy.wait()
    for copy in large[2:]:
        copy.start()
    for d in range(4):
        spread[32 * d : 32 * d + 25, :] = quarters[d]
    me = lax.axis_index(("x_hi", "core"))
    into, at = (lax.broadcasted_iota(jnp.int32, (NO, 128), axis) for axis in (0, 1))
    place = jnp.where((into == 25 * (me ^ (at // 32)) + at % 32) & (at % 32 < 25), 1.0, 0.0).astype(BF16)
    amps[...] = jnp.dot(place, spread[...], preferred_element_type=F32).astype(BF16)
    window[...] = jnp.dot(pick, amps[...], preferred_element_type=F32).astype(BF16)

    lane = lax.broadcasted_iota(jnp.int32, (32, WIDE), 1)

    def scatter(p, q):
        low = min(QUARTER * q // 128 * 128, 512)
        for t in range(3):
            block, s = divmod(4 * t + q, 3)
            shift = (offset_of(s) - (QUARTER * q - low)) % 512
            part = wide[p % 2, 32 * t : 32 * (t + 1), low : low + 512]
            if shift:
                part = pltpu.roll(part, shift, 1)
            if s:
                part = jnp.where(lane >= offset_of(s), part[:, :WIDE], part[:, WIDE:])
            else:
                part = part[:, :WIDE]
            start = BLOCK * block + (8 * s + p if p < 8 else 16 + 2 * s + p)
            for half in range(2):
                blocks[half, pl.ds(start, 32, stride=128), :] = part[:, 128 * half : 128 * (half + 1)]

    for p in range(LOCAL):
        large[p].wait()
        for n in range(4):
            cols = slice(WIDE * n, min(WIDE * (n + 1), NV))
            direct = lax.dot_general(
                window[...], vv[p, cols, :], (((1,), (1,)), ((), ())), preferred_element_type=F32
            )
            hole = jnp.dot(holes[p], amps[:, cols], preferred_element_type=F32)
            wide[p % 2, :, cols] = direct - hole
            if p:
                scatter(p - 1, n)
    for n in range(4):
        scatter(LOCAL - 1, n)

    sends = []
    for chunk in range(8):
        for to in range(16 * chunk, 16 * (chunk + 1)):
            core, z, y, x_hi, x_lo = to // 64, to // 16 % 4, to // 4 % 4, to // 2 % 2, to % 2
            at = BLOCK * (x_hi * 64 + core * 32 + z * 8 + y * 2 + x_lo)
            for half in range(2):
                out[to, :, 128 * half : 128 * (half + 1)] = blocks[half, at : at + BLOCK, :].astype(BF16)
        piece = pl.ds(16 * chunk, 16)
        sends.append(pltpu.make_async_copy(out.at[piece], out_hbm.at[piece], out_sem.at[chunk]))
        sends[-1].start()
    for copy in sends:
        copy.wait()


def dress(vv_vectors, holes, quarters):
    anywhere = pl.BlockSpec(memory_space=pl.ANY)
    held = pl.BlockSpec(memory_space=pltpu.HBM)
    return pl.pallas_call(
        dress_kernel,
        out_shape=jax.ShapeDtypeStruct((DEVICES, BLOCK, WIDE), BF16),
        in_specs=[held, held] + [anywhere] * 4,
        out_specs=held,
        scratch_shapes=[
            pltpu.VMEM((LOCAL, NV, NV), BF16),
            pltpu.VMEM((LOCAL, I_ROWS, NO), BF16),
            pltpu.VMEM((4, 25, NV), BF16),
            pltpu.VMEM((128, NV), BF16),
            pltpu.VMEM((NO, NV), BF16),
            pltpu.VMEM((I_ROWS, NV), BF16),
            pltpu.VMEM((2, I_ROWS, 1024), F32),
            pltpu.VMEM((2, DEVICES * BLOCK, 128), F32),
            pltpu.VMEM((DEVICES, BLOCK, WIDE), BF16),
            pltpu.SemaphoreType.DMA((LOCAL,)),
            pltpu.SemaphoreType.DMA((5,)),
            pltpu.SemaphoreType.DMA((8,)),
        ],
        compiler_params=pltpu.CompilerParams(vmem_limit_bytes=DRESS_VMEM),
        cost_estimate=pl.CostEstimate(
            flops=2 * LOCAL * I_ROWS * NV * NV, bytes_accessed=2 * LOCAL * NV * NV, transcendentals=0
        ),
        name="dress",
    )(vv_vectors, holes, *quarters)


def order_kernel(mine_ref, other_ref, out_ref, tail):
    me_z, me_y, me_x, me_core = (lax.axis_index(a) for a in ("z", "y", ("x_hi", "x_lo"), "core"))

    def place(chip):
        z, y, x = chip // 16, chip // 4 % 4, chip % 4
        return (me_x + 4 - x) % 4 * 16 + (me_y + 4 - y) % 4 * 4 + (me_z + 4 - z) % 4

    @pl.loop(0, DEVICES // 4)
    def _(pair):
        halves = [(mine_ref[at].astype(F32), other_ref[at].astype(F32)) for at in (place(2 * pair), place(2 * pair + 1))]
        for core in range(2):
            one, two = (jnp.where(me_core == core, mine, other) for mine, other in halves)
            rows = pl.ds(pl.multiple_of(core * 512 + pair * 16, 16), 16)
            for c in range(8):
                both = jnp.concatenate([one[8 * c : 8 * c + 8], two[8 * c : 8 * c + 8]], axis=0)
                out_ref[rows, 128 * c : 128 * (c + 1)] = both.astype(BF16)
            start = pl.multiple_of(core * 1024 + pair * 32, 32)
            tail[pl.ds(start, 16), :] = one[64:80]
            tail[pl.ds(start + 16, 16), :] = two[64:80]

    for e in range(2):
        for c in range(8):
            out_ref[1024 + 128 * e : 1152 + 128 * e, 128 * c : 128 * (c + 1)] = tail[
                pl.ds(8 * e + c, DEVICES, stride=16), :
            ].astype(BF16)


def ordered(mine, other):
    return pl.pallas_call(
        order_kernel,
        out_shape=jax.ShapeDtypeStruct((1280, SLAB), BF16),
        scratch_shapes=[pltpu.VMEM((2048, 128), F32)],
        compiler_params=pltpu.CompilerParams(vmem_limit_bytes=16 * 1024 * 1024),
        cost_estimate=pl.CostEstimate(flops=0, bytes_accessed=6 * 1024 * 1024, transcendentals=0),
        name="ordered",
    )(mine, other)


def contract_kernel(blocks_ref, slab_ref, out_ref, dressed, tail):
    GROUP = 16
    m = pl.program_id(0)
    after = jnp.minimum(m + 1, 2)
    limit = jnp.where(m < 2, 250 - 6 * m, WIDE)

    @pl.when(m == 0)
    def _():
        @pl.loop(0, DEVICES // GROUP, unroll=2)
        def _(g):
            group = pl.ds(g * GROUP, GROUP)
            rows = pl.ds(pl.multiple_of(g * GROUP * 8, GROUP * 8), GROUP * 8)
            for half in range(2):
                part = blocks_ref[group, 24:32, 128 * half : 128 * (half + 1)]
                tail[half, rows, :] = part.astype(F32).reshape(GROUP * 8, 128)

    lane = lax.broadcasted_iota(jnp.int32, (GROUP * 8, WIDE), 1)

    @pl.loop(0, DEVICES // GROUP, unroll=2)
    def _(g):
        group = pl.ds(g * GROUP, GROUP)
        rows = pl.ds(pl.multiple_of(g * GROUP * 8, GROUP * 8), GROUP * 8)
        one, two = (
            blocks_ref[group, pl.ds(pl.multiple_of(8 * s, 8), 8), :].astype(F32).reshape(GROUP * 8, WIDE)
            for s in (m, after)
        )
        dressed[rows, :] = jnp.where(lane < limit, one, two).astype(BF16)

    lanes = lax.broadcasted_iota(jnp.int32, (DEVICES, 128), 1)
    for e in range(2):
        rows = slice(1024 + 128 * e, 1152 + 128 * e)
        for half in range(2):
            one, two = (tail[half, pl.ds(2 * s + e, DEVICES, stride=8), :] for s in (m, after))
            dressed[rows, 128 * half : 128 * (half + 1)] = jnp.where(
                lanes + 128 * half < limit, one, two
            ).astype(BF16)

    out_ref[...] = lax.dot_general(
        dressed[...], slab_ref[...], (((0,), (0,)), ((), ())), preferred_element_type=F32
    )


def contract(blocks, slab):
    return pl.pallas_call(
        contract_kernel,
        grid=(3,),
        out_shape=jax.ShapeDtypeStruct((750, SLAB), F32),
        in_specs=[
            pl.BlockSpec(memory_space=pltpu.VMEM),
            pl.BlockSpec(memory_space=pltpu.VMEM),
        ],
        out_specs=pl.BlockSpec((WIDE, SLAB), lambda m: (m, 0)),
        scratch_shapes=[pltpu.VMEM((1280, WIDE), BF16), pltpu.VMEM((2, 1024, 128), F32)],
        compiler_params=pltpu.CompilerParams(
            dimension_semantics=("arbitrary",), vmem_limit_bytes=32 * 1024 * 1024
        ),
        cost_estimate=pl.CostEstimate(
            flops=2 * 768 * 1280 * SLAB, bytes_accessed=8 * 1024 * 1024, transcendentals=0
        ),
        name="contract",
    )(blocks, slab)


def slab_kernel(slab_ref, out_ref, rows):
    for c in range(8):
        part = slab_ref[:, 128 * c : 128 * (c + 1)].astype(F32)
        rows[8 * c : 8 * c + 8, :] = part[0:8]
        for e in range(2):
            rows[64 + 8 * e + c : 65 + 8 * e + c, :] = part[8 + e : 9 + e]
    out_ref[...] = rows[...].astype(BF16)


def slab_rows(ov_slab):
    return pl.pallas_call(
        slab_kernel,
        out_shape=jax.ShapeDtypeStruct((80, 128), BF16),
        scratch_shapes=[pltpu.VMEM((80, 128), F32)],
        compiler_params=pltpu.CompilerParams(vmem_limit_bytes=4 * 1024 * 1024),
        cost_estimate=pl.CostEstimate(flops=0, bytes_accessed=64 * 1024, transcendentals=0),
        name="slab_rows",
    )(ov_slab)


def round_axis(rows, axis):
    others = [lax.ppermute(rows, axis, [(i, (i + d) % 4) for i in range(4)]) for d in (1, 2, 3)]
    return jnp.concatenate([rows, *others], axis=0)


def shards(vv_vectors, oo_vectors, ov_slab, amplitudes):
    group = ("x_hi", "core")
    quarters = [amplitudes] + [lax.ppermute(amplitudes, group, [(i, i ^ d) for i in range(4)]) for d in (1, 2, 3)]
    rows = round_axis(slab_rows(ov_slab), "z")
    rows, oo_vectors = lax.optimization_barrier((rows, oo_vectors))
    holes = hole_factors(oo_vectors)
    rows, holes, quarters = lax.optimization_barrier((rows, holes, quarters))
    rows = round_axis(rows, "y")
    blocks = dress(vv_vectors, holes, quarters)
    rows, blocks = lax.optimization_barrier((rows, blocks))
    blocks = lax.all_to_all(blocks, RING, split_axis=0, concat_axis=0, tiled=True)
    rows = round_axis(rows, ("x_hi", "x_lo"))
    other = lax.ppermute(rows, "core", [(0, 1), (1, 0)])
    return contract(blocks, ordered(rows.reshape(64, 80, 128), other.reshape(64, 80, 128)))


def solution(mesh):
    split = Mesh(mesh.devices.reshape(2, 2, 4, 4, 2), AXES)
    return jax.shard_map(
        shards,
        mesh=split,
        in_specs=(P(AXES, None, None), P(AXES, None, None), P(AXES, None), P(("x_hi", "core"), None)),
        out_specs=P(AXES, None),
        check_vma=False,
    )
```
